32 devices in a mesh: lvl: 4 (over z), gx: 4 (over y, core), gy: 2 (over x).
Axes of the slice: x: 2, y: 2, z: 4, core: 2. Of those that a mesh axis runs over, the one named last changes fastest.
Arguments:
- initial: float32 [256, 256, 256], P('gx', 'gy'), may hold values from -6 to 6
- reaction: float32 [256, 256, 256], P('gx', 'gy'), may hold values from -0.5 to 0
Outputs:
- levels: float32 [4, 256, 256, 256], P('lvl', 'gx', 'gy')
The draws below stay inside these ranges and needn't reach their ends.
All inputs are finite; a program needn't handle non-finite values.
Results may differ from the reference program's by a relative error of at most 0.0001.
Values sent between devices are 32-bit elements; how exact they have to be, the bound alone decides.
No kernel may reach another device: no remote copies, remote signals or barrier semaphores. Data moves between devices by JAX's collectives and lax.ppermute only.
A program may use at most 64 MiB of HBM per device.

```python
import jax
import jax.numpy as jnp

NX = 256
NY = 256
NZ = 256
STEPS = 1
KX = 128
KY = 128
KZ = 64
N_LVL = 4


def shard_levels(stream_key, extent, split, low, largest):
    def one(axis_at, blocks):
        heights = jax.random.uniform(jax.random.fold_in(jax.random.fold_in(stream_key, 6), axis_at), (blocks,), jnp.float32, low / len(split), largest / len(split))
        return jnp.repeat(jnp.exp(heights), extent[axis_at] // blocks).reshape((-1,) + (1,) * (len(extent) - axis_at - 1))

    gain = one(*split[0])
    for cut in split[1:]:
        gain = gain * one(*cut)
    return gain


def gaussian(key, extent, spread, bound, pieces=(), dtype=jnp.bfloat16):
    values = spread * jax.random.normal(key, extent, jnp.float32)
    if pieces:
        values = values * shard_levels(key, extent, pieces, -0.22, 0.18)
    return jnp.clip(values, -bound, bound).astype(dtype)


def setup_inputs(seed: int = 0) -> dict:
    streams_of = jax.random.split(jax.random.key(seed), 3)
    initial = gaussian(streams_of[0], (NX, NY, NZ), 1.0, 6.0, ((0, 4), (1, 2)), jnp.float32)
    reaction = jnp.clip(-0.5 + 0.5 * jax.random.uniform(streams_of[1], (NX, NY, NZ), jnp.float32) ** shard_levels(streams_of[1], (NX, NY, NZ), ((0, 4), (1, 2)), -0.2, 0.2), -0.5, 0.0)
    return {"initial": initial, "reaction": reaction}


DIFFUSE = 0.3


def evaluate(grid_field, reaction):
    spectrum = jnp.fft.rfftn(grid_field)
    index_x = (jnp.arange(KX) - KX // 2) % NX
    index_y = (jnp.arange(KY) - KY // 2) % NY
    index_z = jnp.arange(KZ)
    kept = spectrum[index_x][:, index_y][:, :, :KZ]
    wave_x = ((jnp.arange(KX) - KX // 2).astype(jnp.float32) / (NX // 4))[:, None, None]
    wave_y = ((jnp.arange(KY) - KY // 2).astype(jnp.float32) / (NY // 4))[None, :, None]
    wave_z = (jnp.arange(KZ).astype(jnp.float32) / (NZ // 4))[None, None, :]
    factor_real = -DIFFUSE * (wave_x * wave_x + wave_y * wave_y + wave_z * wave_z)
    factor_imag = -(0.3 * wave_x + 0.2 * wave_y + 0.25 * wave_z)
    scaled = kept * (factor_real + 1j * factor_imag)
    filled = jnp.zeros_like(spectrum).at[index_x[:, None, None], index_y[None, :, None], index_z[None, None, :]].set(scaled)
    values = jnp.fft.irfftn(filled, s=(NX, NY, NZ)).astype(jnp.float32)
    return values + reaction * grid_field


def reference(initial, reaction):
    previous = None
    finals = []
    for level_index in range(N_LVL):
        current = initial
        terms = [evaluate(current, reaction)]
        for position in range(STEPS):
            update = current + terms[position]
            if previous is not None:
                update = update + 0.5 * (previous[position + 1] - previous[position])
            current = update
            terms.append(evaluate(current, reaction))
        finals.append(current)
        previous = terms
    return jnp.stack(finals)
```

```python
import math

import jax
import jax.numpy as jnp
from jax import lax
from jax.sharding import PartitionSpec as P

DIFFUSE = 0.3
PRECISION = lax.Precision.HIGH


def cos_sin(points, waves, length):
    turns = points[:, None] * waves[None, :] % length
    angles = turns.astype(jnp.float32) * (2.0 * math.pi / length)
    return jnp.cos(angles), jnp.sin(angles)


def complex_table(cosine, sine, direction):
    turned = direction * sine
    return jnp.stack([jnp.stack([cosine, turned], axis=1), jnp.stack([-turned, cosine], axis=1)])


def contract(spec, left, right):
    return jnp.einsum(spec, left, right, precision=PRECISION)


def swap(block, axes, mask):
    count = lax.axis_size(axes)
    return lax.ppermute(block, axes, [(i, i ^ mask) for i in range(count)])


def iota(count):
    return lax.broadcasted_iota(jnp.int32, (count,), 0)


def shards(initial, reaction):
    rows_x, rows_y, depth = initial.shape
    parts_x = lax.axis_size("gx")
    parts_y = lax.axis_size("gy")
    levels = lax.axis_size("lvl")
    full_x, full_y = rows_x * parts_x, rows_y * parts_y
    modes_x, modes_y, modes_z = full_x // 2, full_y // 2, depth // 4
    norm = 1.0 / (full_x * full_y * depth)
    level, at_x, at_y = (lax.axis_index(a) for a in ("lvl", "gx", "gy"))

    pair = at_x & 1
    extra = [("gx", 1 << k) for k in range(2, parts_x.bit_length() - 1)]
    extra += [("gy", 1 << k) for k in range(1, parts_y.bit_length() - 1)]
    place = ((at_x >> 1) & 1) * 2 + (at_y & 1)
    for axis, mask in extra:
        place = place * 2 + (lax.axis_index(axis) // mask & 1)
    blocks = parts_x // 2 * parts_y
    block_x = modes_x // blocks
    block_z = modes_z // levels
    half_z = block_z // 2

    waves_x = iota(modes_x)
    waves_x = ((waves_x // block_x) ^ place) * block_x + waves_x % block_x - modes_x // 2
    waves_y = iota(modes_y) - modes_y // 2
    near = pair * half_z + iota(half_z)
    far = (1 - pair) * half_z + iota(half_z)
    points_x = jnp.concatenate([at_x * rows_x + iota(rows_x), (at_x ^ 1) * rows_x + iota(rows_x)])
    points_y = at_y * rows_y + iota(rows_y)

    cosine, sine = cos_sin(jnp.concatenate([near, far]) + level * block_z, iota(depth), depth)
    forward_z = jnp.stack([cosine, -sine], axis=1).reshape(2, half_z, 2, depth)
    cosine_y, sine_y = cos_sin(points_y, waves_y, full_y)
    forward_y = complex_table(cosine_y, sine_y, -1.0)
    cosine_x, sine_x = cos_sin(points_x, waves_x, full_x)
    forward_x = complex_table(cosine_x, sine_x, -1.0)
    back_x = complex_table(cosine_x.T, sine_x.T, 1.0)
    back_y = complex_table(cosine_y.T, sine_y.T, 1.0)
    lots = [(level ^ m) * block_z for m in range(levels)]
    waves_z = jnp.concatenate([lot + near for lot in lots] + [lot + far for lot in lots])
    cosine, sine = cos_sin(waves_z, iota(depth), depth)
    weights = jnp.where(waves_z == 0, 1.0, 2.0).astype(jnp.float32)[:, None]
    back_z = jnp.stack([cosine * weights, -sine * weights], axis=1)

    own_z = (level * block_z + near)[:, None, None]
    own_x = waves_x[:block_x][None, :, None]
    own_y = waves_y[None, None, :]
    unit_x = own_x.astype(jnp.float32) / (full_x // 4)
    unit_y = own_y.astype(jnp.float32) / (full_y // 4)
    unit_z = own_z.astype(jnp.float32) / (depth // 4)
    factor_real = -DIFFUSE * (unit_x * unit_x + unit_y * unit_y + unit_z * unit_z) * norm
    factor_imag = -(0.3 * unit_x + 0.2 * unit_y + 0.25 * unit_z) * norm
    edge = (own_z == 0) & ((own_x == -(modes_x // 2)) | (own_y == -(modes_y // 2)))
    again = jnp.where(edge, 0.5, 1.0).astype(jnp.float32)[:, None] / norm

    def forward(field):
        planes = contract("hkpz,xyz->hkpxy", forward_z, field)
        other = swap(planes[1], "gx", 1)
        planes = jnp.concatenate([planes[0], other], axis=2)
        planes = contract("kpxy,pyqm->kqxm", planes, forward_y)
        planes = contract("kpxm,pxqj->kqjm", planes, forward_x)
        quarter = modes_x // 4
        pieces = [planes[:, :, i * quarter : (i + 1) * quarter] for i in range(4)]
        total = pieces[0] + swap(pieces[1], "gy", 1) + swap(pieces[2], "gx", 2)
        total = total + swap(pieces[3], ("gx", "gy"), 2 * parts_y + 1)
        for axis, mask in extra:
            middle = total.shape[2] // 2
            total = total[:, :, :middle] + swap(total[:, :, middle:], axis, mask)
        return total

    def scaled(spectrum):
        real, imag = spectrum[:, 0], spectrum[:, 1]
        return jnp.stack(
            [
                factor_real * real - factor_imag * imag,
                factor_real * imag + factor_imag * real,
            ],
            axis=1,
        )

    def gather(piece):
        for axis, mask in reversed(extra):
            piece = jnp.concatenate([piece, swap(piece, axis, mask)], axis=2)
        found = []
        for m in range(levels):
            lot = piece if m == 0 else swap(piece, "lvl", m)
            by_y = swap(lot, "gy", 1)
            by_x = swap(lot, "gx", 2)
            cross = swap(by_y, "gx", 2) if m % 2 == 0 else swap(by_x, "gy", 1)
            found.append([lot, by_y, by_x, cross])
        return found

    def back(found):
        modes = jnp.concatenate([jnp.concatenate(lot, axis=2) for lot in found], axis=0)
        lines = contract("npjm,pjqx->nqxm", modes, back_x)
        lines = contract("npxm,pmqy->nqxy", lines, back_y)
        other = swap(lines[:, :, rows_x:], "gx", 1)
        lines = jnp.concatenate([lines[:, :, :rows_x], other], axis=0)
        return contract("npxy,npz->xyz", lines, back_z)

    first = scaled(forward(initial))
    first_found = gather(first)
    second = scaled(again * first + forward(reaction * initial))
    second_found = gather(second)
    rate = back(first_found) + reaction * initial
    third = scaled(again * second + forward(reaction * rate))
    third_found = gather(third)
    rate_again = back(second_found) + reaction * rate
    fourth = scaled(again * third + forward(reaction * rate_again))
    fourth_found = gather(fourth)
    total = initial + rate + jnp.where(level >= 1, 0.5, 0.0) * rate_again
    rate_third = back(third_found) + reaction * rate_again
    rate_fourth = back(fourth_found) + reaction * rate_third
    total = total + jnp.where(level >= 2, 0.25, 0.0) * rate_third
    total = total + jnp.where(level >= 3, 0.125, 0.0) * rate_fourth
    return total[None]


def solution(mesh):
    in_specs = (P("gx", "gy", None), P("gx", "gy", None))
    out_specs = P("lvl", "gx", "gy", None)
    return jax.shard_map(shards, mesh=mesh, in_specs=in_specs, out_specs=out_specs, check_vma=False)
```

```python
import functools
import math

import jax
import jax.numpy as jnp
from jax import lax
from jax.experimental import pallas as pl
from jax.experimental.pallas import tpu as pltpu
from jax.sharding import PartitionSpec as P

DIFFUSE = 0.3
PRECISION = lax.Precision.HIGH
LANES = 128
SLAB = 8
F32 = jnp.float32
VMEM = pl.BlockSpec(memory_space=pltpu.VMEM)


def cos_sin(points, waves, length):
    turns = points[:, None] * waves[None, :] % length
    angles = turns.astype(F32) * (2.0 * math.pi / length)
    return jnp.cos(angles), jnp.sin(angles)


def complex_table(cosine, sine, direction):
    turned = direction * sine
    return jnp.stack([jnp.stack([cosine, turned], axis=1), jnp.stack([-turned, cosine], axis=1)])


def contract(spec, left, right):
    return jnp.einsum(spec, left, right, precision=PRECISION)


def swap(block, axes, mask):
    count = lax.axis_size(axes)
    return lax.ppermute(block, axes, [(i, i ^ mask) for i in range(count)])


def iota(count):
    return lax.broadcasted_iota(jnp.int32, (count,), 0)


def split_table(table):
    high = lax.reduce_precision(table, 8, 7)
    return high.astype(jnp.bfloat16), (table - high).astype(jnp.bfloat16)


def split(value):
    high = value.astype(jnp.bfloat16)
    return high, (value - high.astype(F32)).astype(jnp.bfloat16)


def dot(left, right):
    return jnp.dot(left, right, preferred_element_type=F32)


def dot_turned(left, right):
    return lax.dot_general(left, right, (((1,), (1,)), ((), ())), preferred_element_type=F32)


def right_table(value, high, low):
    value_high, value_low = split(value)
    rows = value.shape[0]
    both = dot(jnp.concatenate([value_high, value_low], axis=0), high)
    return both[:rows] + both[rows:] + dot(value_high, low)


def left_table(stacked, high, value):
    value_high, value_low = split(value)
    rows = high.shape[0]
    both = dot(stacked, value_high)
    return both[:rows] + both[rows:] + dot(high, value_low)


def analyze_rows(stacked, field, near, far):
    lines, count, depth = field.shape
    waves = stacked.shape[0] // 2
    for at in range(0, lines, 2):
        pair_high, pair_low = split(field[at : at + 2].reshape(2 * count, depth))
        both = dot_turned(stacked, pair_high)
        waves_at = both[:waves] + both[waves:] + dot_turned(stacked[:waves], pair_low)
        for i in range(2):
            part = waves_at[:, i * count : (i + 1) * count]
            near[at + i] = part[: waves // 2]
            far[at + i] = part[waves // 2 :]


def analyze_kernel(table, field, near, far):
    analyze_rows(table[...], field[...], near, far)


def analyze_product_kernel(table, field, reaction, near, far):
    analyze_rows(table[...], field[...] * reaction[...], near, far)


def plane_kernel(table_y_high, table_y_low, table_x, table_x_high, near, other, *out):
    half = near.shape[0]
    waves, _, quarter, modes_y = out[0].shape
    stride = 2 * waves
    rows = half // stride

    @pl.loop(0, waves)
    def _(k):
        parts = []
        for p in range(2):
            lines = [r[pl.ds(p * waves + k, rows, stride=stride), :] for r in (near, other)]
            parts.append(jnp.concatenate(lines, axis=0))
        lines = jnp.concatenate(parts, axis=1)
        lines = right_table(lines, table_y_high[...], table_y_low[...])
        lines = jnp.concatenate([lines[:, :modes_y], lines[:, modes_y:]], axis=0)
        modes = left_table(table_x[...], table_x_high[...], lines)
        for j, ref in enumerate(out):
            for p in range(2):
                at = (2 * j + p) * quarter
                ref[k, p] = modes[at : at + quarter]


def lines_kernel(table_x, table_x_high, table_y_high, table_y_low, *refs):
    lots, by_y, by_x, cross_first, cross_second, own, send = refs
    waves, _, quarter, modes_y = cross_first.shape
    _, _, rows_x, rows_y = own.shape

    @pl.loop(0, waves)
    def _(k):
        columns = []
        for lot, cross in enumerate((cross_first, cross_second)):
            n = lot * waves + k
            pieces = [lots[n], by_y[n], by_x[n], cross[k]]
            pieces = [piece.reshape(2 * quarter, modes_y) for piece in pieces]
            columns.append(jnp.concatenate(pieces, axis=0))
        lines = left_table(table_x[...], table_x_high[...], jnp.concatenate(columns, axis=1))
        middle = lines.shape[0] // 2
        rows = []
        for lot in range(2):
            part = lines[:, lot * modes_y : (lot + 1) * modes_y]
            rows.append(jnp.concatenate([part[:middle], part[middle:]], axis=1))
        planes = right_table(jnp.concatenate(rows, axis=0), table_y_high[...], table_y_low[...])
        for lot in range(2):
            for q in range(2):
                part = planes[lot * middle : (lot + 1) * middle, q * rows_y : (q + 1) * rows_y]
                own[lot * waves + k, q] = part[:rows_x]
                send[lot * waves + k, q] = part[rows_x:]


def synthesize_rows(high, low, planes):
    lines = planes[0].shape[1]
    stacked = jnp.concatenate([high, high], axis=0)
    flat = [plane.reshape(plane.shape[0] * lines, plane.shape[2]) for plane in planes]
    for at in range(lines):
        waves = [ref[pl.ds(at, ref.shape[0] // lines, stride=lines), :] for ref in flat]
        value_high, value_low = split(jnp.concatenate(waves, axis=0).T)
        both = jnp.concatenate([value_high, value_low], axis=1)
        yield at, dot(both, stacked) + dot(value_high, low)


def rate_kernel(groups, table_high, table_low, table, reaction, before, *refs):
    planes, (rate, near, far) = refs[:groups], refs[groups:]
    for at, value in synthesize_rows(table_high[...], table_low[...], planes):
        rate[at] = value + reaction[at] * before[at]
    analyze_rows(table[...], reaction[...] * rate[...], near, far)


def total_kernel(groups, table_high, table_low, share, reaction, initial, first, second, *refs):
    planes, (total,) = refs[:groups], refs[groups:]
    for at, value in synthesize_rows(table_high[...], table_low[...], planes):
        third = value + reaction[at] * second[at]
        early = initial[at] + first[at] + share[0] * second[at]
        total[at] = early + (share[1] + share[2] * reaction[at]) * third


def last_kernel(groups, table_high, table_low, share, before, *refs):
    planes, (total,) = refs[:groups], refs[groups:]
    for at, value in synthesize_rows(table_high[...], table_low[...], planes):
        total[at] = before[at] + share[2] * value


def shards(initial, reaction):
    rows_x, rows_y, depth = initial.shape
    parts_x = lax.axis_size("gx")
    parts_y = lax.axis_size("gy")
    levels = lax.axis_size("lvl")
    full_x, full_y = rows_x * parts_x, rows_y * parts_y
    modes_x, modes_y, modes_z = full_x // 2, full_y // 2, depth // 4
    norm = 1.0 / (full_x * full_y * depth)
    level, at_x, at_y = (lax.axis_index(a) for a in ("lvl", "gx", "gy"))

    pair = at_x & 1
    extra = [("gx", 1 << k) for k in range(2, parts_x.bit_length() - 1)]
    extra += [("gy", 1 << k) for k in range(1, parts_y.bit_length() - 1)]
    place = ((at_x >> 1) & 1) * 2 + (at_y & 1)
    for axis, mask in extra:
        place = place * 2 + (lax.axis_index(axis) // mask & 1)
    blocks = parts_x // 2 * parts_y
    block_x = modes_x // blocks
    quarter = modes_x // 4
    block_z = modes_z // levels
    half_z = block_z // 2
    groups = levels // 2

    waves_x = iota(modes_x)
    waves_x = ((waves_x // block_x) ^ place) * block_x + waves_x % block_x - modes_x // 2
    waves_y = iota(modes_y) - modes_y // 2
    near_z = pair * half_z + iota(half_z)
    far_z = (1 - pair) * half_z + iota(half_z)
    points_x = jnp.concatenate([at_x * rows_x + iota(rows_x), (at_x ^ 1) * rows_x + iota(rows_x)])
    points_y = at_y * rows_y + iota(rows_y)

    cosine, sine = cos_sin(jnp.concatenate([near_z, far_z]) + level * block_z, iota(depth), depth)
    forward_z = jnp.stack([cosine.reshape(2, half_z, depth), -sine.reshape(2, half_z, depth)], axis=1)
    forward_z = forward_z.reshape(4 * half_z, depth)
    cosine_y, sine_y = cos_sin(points_y, waves_y, full_y)
    forward_y = complex_table(cosine_y, sine_y, -1.0)
    cosine_x, sine_x = cos_sin(points_x, waves_x, full_x)
    forward_x = complex_table(cosine_x, sine_x, -1.0)
    back_x = complex_table(cosine_x.T, sine_x.T, 1.0)
    back_y = complex_table(cosine_y.T, sine_y.T, 1.0)
    waves_z = []
    for group in range(groups):
        for half in (near_z, far_z):
            for lot in range(2):
                waves_z.append((level ^ (2 * group + lot)) * block_z + half)
    waves_z = jnp.concatenate(waves_z)
    cosine, sine = cos_sin(waves_z, iota(depth), depth)
    weights = jnp.where(waves_z == 0, 1.0, 2.0).astype(F32)[:, None]
    back_z = jnp.stack([cosine * weights, -sine * weights], axis=1)
    back_z = back_z.reshape(2 * modes_z, depth)

    own_z = (level * block_z + near_z)[:, None, None]
    own_x = waves_x[:block_x][None, :, None]
    own_y = waves_y[None, None, :]
    unit_x = own_x.astype(F32) / (full_x // 4)
    unit_y = own_y.astype(F32) / (full_y // 4)
    unit_z = own_z.astype(F32) / (depth // 4)
    factor_real = -DIFFUSE * (unit_x * unit_x + unit_y * unit_y + unit_z * unit_z) * norm
    factor_imag = -(0.3 * unit_x + 0.2 * unit_y + 0.25 * unit_z) * norm
    edge = (own_z == 0) & ((own_x == -(modes_x // 2)) | (own_y == -(modes_y // 2)))
    again = jnp.where(edge, 0.5, 1.0).astype(F32)[:, None] / norm
    share = [
        jnp.where(level >= k, jnp.float32(2.0**-k), jnp.float32(0.0)) for k in range(1, levels)
    ]

    tiled = rows_y % LANES == 0 and depth % LANES == 0 and rows_x % SLAB == 0
    tiled = tiled and half_z % SLAB == 0 and modes_y % LANES == 0 and quarter % SLAB == 0

    if tiled:
        steps = rows_x // SLAB
        grid_spec = pl.BlockSpec((SLAB, rows_y, depth), lambda s: (s, 0, 0))
        wave_spec = pl.BlockSpec((SLAB, 2 * half_z, rows_y), lambda s: (s, 0, 0))
        plane_spec = pl.BlockSpec((4 * half_z, SLAB, rows_y), lambda s: (0, s, 0))
        share_spec = pl.BlockSpec(memory_space=pltpu.SMEM)
        grid_shape = jax.ShapeDtypeStruct((rows_x, rows_y, depth), F32)
        wave_shape = jax.ShapeDtypeStruct((rows_x, 2 * half_z, rows_y), F32)
        waves_stacked = jnp.concatenate(split_table(forward_z), axis=0)
        back_high, back_low = split_table(back_z)
        x_table = forward_x.reshape(2, 2 * rows_x, 2, 4, quarter).transpose(3, 2, 4, 0, 1)
        x_table = x_table.reshape(8 * quarter, 4 * rows_x)
        x_high, x_low = split_table(x_table)
        x_stacked = jnp.concatenate([x_high, x_low], axis=0)
        y_high, y_low = split_table(forward_y.reshape(2 * rows_y, 2 * modes_y))
        x_back = back_x.reshape(2, 4, quarter, 2, 2 * rows_x).transpose(3, 4, 1, 0, 2)
        x_back = x_back.reshape(4 * rows_x, 8 * quarter)
        x_back_high, x_back_low = split_table(x_back)
        x_back_stacked = jnp.concatenate([x_back_high, x_back_low], axis=0)
        y_back_high, y_back_low = split_table(back_y.reshape(2 * modes_y, 2 * rows_y))
        share_array = jnp.stack(share)

        def whole(array):
            return pl.BlockSpec(array.shape, lambda s: (0,) * array.ndim)

        def by_slab(kernel, tables, blocks, out_shape, out_specs):
            specs = []
            for block in blocks:
                if block.shape == grid_shape.shape:
                    specs.append(grid_spec)
                else:
                    specs.append(plane_spec)
            table_specs = [share_spec if t is share_array else whole(t) for t in tables]
            moved = sum(math.prod(b.shape) for b in blocks) * 4
            return pl.pallas_call(
                kernel,
                grid=(steps,),
                in_specs=table_specs + specs,
                out_specs=out_specs,
                out_shape=out_shape,
                cost_estimate=pl.CostEstimate(
                    flops=12 * modes_z * rows_x * rows_y * depth,
                    bytes_accessed=moved,
                    transcendentals=0,
                ),
            )(*tables, *blocks)

        def analyze(field):
            return by_slab(
                analyze_kernel, [waves_stacked], [field], [wave_shape] * 2, [wave_spec] * 2
            )

        def analyze_product(field):
            return by_slab(
                analyze_product_kernel,
                [waves_stacked],
                [field, reaction],
                [wave_shape] * 2,
                [wave_spec] * 2,
            )

        def plane_waves(near, other):
            flat = (rows_x * 2 * half_z, rows_y)
            piece = jax.ShapeDtypeStruct((half_z, 2, quarter, modes_y), F32)
            return pl.pallas_call(
                plane_kernel,
                in_specs=[VMEM] * 6,
                out_specs=[VMEM] * 4,
                out_shape=[piece] * 4,
                cost_estimate=pl.CostEstimate(
                    flops=24 * half_z * modes_x * modes_y * 2 * (rows_x + rows_y),
                    bytes_accessed=4 * half_z * modes_x * modes_y * 4,
                    transcendentals=0,
                ),
            )(y_high, y_low, x_stacked, x_high, near.reshape(flat), other.reshape(flat))

        def plane_lines(found):
            shape = jax.ShapeDtypeStruct((2 * half_z, 2, rows_x, rows_y), F32)
            own, send = pl.pallas_call(
                lines_kernel,
                in_specs=[VMEM] * 9,
                out_specs=[VMEM] * 2,
                out_shape=[shape] * 2,
                cost_estimate=pl.CostEstimate(
                    flops=48 * half_z * modes_x * modes_y * 2 * (rows_x + rows_y),
                    bytes_accessed=8 * half_z * modes_x * modes_y * 4,
                    transcendentals=0,
                ),
            )(x_back_stacked, x_back_high, y_back_high, y_back_low, *found)
            return own, send

        def flat_planes(planes):
            return [p.reshape(4 * half_z, rows_x, rows_y) for p in planes]

        def next_rate(planes, before):
            planes = flat_planes(planes)
            return by_slab(
                functools.partial(rate_kernel, len(planes)),
                [back_high, back_low, waves_stacked],
                [reaction, before, *planes],
                [grid_shape, wave_shape, wave_shape],
                [grid_spec, wave_spec, wave_spec],
            )

        def total_before(planes, first, second):
            planes = flat_planes(planes)
            return by_slab(
                functools.partial(total_kernel, len(planes)),
                [back_high, back_low, share_array],
                [reaction, initial, first, second, *planes],
                grid_shape,
                grid_spec,
            )

        def total_last(planes, before):
            planes = flat_planes(planes)
            return by_slab(
                functools.partial(last_kernel, len(planes)),
                [back_high, back_low, share_array],
                [before, *planes],
                grid_shape,
                grid_spec,
            )

    else:

        def analyze(field):
            waves = contract("kz,xyz->xky", forward_z, field)
            return waves[:, : 2 * half_z], waves[:, 2 * half_z :]

        def analyze_product(field):
            return analyze(field * reaction)

        def plane_waves(near, other):
            lines = jnp.concatenate([near, other], axis=0)
            lines = lines.reshape(2 * rows_x, 2, half_z, rows_y)
            lines = contract("xpky,pyqm->kqxm", lines, forward_y)
            modes = contract("kpxm,pxqj->kqjm", lines, forward_x)
            return [modes[:, :, i * quarter : (i + 1) * quarter] for i in range(4)]

        def plane_lines(found):
            cross = jnp.concatenate(found[3:], axis=0)
            modes = jnp.concatenate([*found[:3], cross], axis=2)
            lines = contract("npjm,pjqx->nqxm", modes, back_x)
            lines = contract("npxm,pmqy->nqxy", lines, back_y)
            return lines[:, :, :rows_x], lines[:, :, rows_x:]

        def grid_field(planes):
            lines = jnp.concatenate(planes, axis=0).reshape(2 * modes_z, rows_x, rows_y)
            return contract("kxy,kz->xyz", lines, back_z)

        def next_rate(planes, before):
            rate = grid_field(planes) + reaction * before
            return rate, *analyze_product(rate)

        def total_before(planes, first, second):
            third = grid_field(planes) + reaction * second
            early = initial + first + share[0] * second
            return early + (share[1] + share[2] * reaction) * third

        def total_last(planes, before):
            return before + share[2] * grid_field(planes)

    def spectrum_of(near, far):
        pieces = plane_waves(near, swap(far, "gx", 1))
        total = pieces[0] + swap(pieces[1], "gy", 1) + swap(pieces[2], "gx", 2)
        total = total + swap(pieces[3], ("gx", "gy"), 2 * parts_y + 1)
        for axis, mask in extra:
            middle = total.shape[2] // 2
            total = total[:, :, :middle] + swap(total[:, :, middle:], axis, mask)
        return total

    def scaled(spectrum):
        real, imag = spectrum[:, 0], spectrum[:, 1]
        return jnp.stack(
            [
                factor_real * real - factor_imag * imag,
                factor_real * imag + factor_imag * real,
            ],
            axis=1,
        )

    def gather(piece):
        for axis, mask in reversed(extra):
            piece = jnp.concatenate([piece, swap(piece, axis, mask)], axis=2)
        lots = [jnp.concatenate([piece, swap(piece, "lvl", 1)], axis=0)]
        mask = 2
        while mask < levels:
            lots += [swap(lot, "lvl", mask) for lot in lots]
            mask *= 2
        found = []
        for lot in lots:
            by_y = swap(lot, "gy", 1)
            by_x = swap(lot, "gx", 2)
            cross_first = swap(by_y[:half_z], "gx", 2)
            cross_second = swap(by_x[half_z:], "gy", 1)
            found.append([lot, by_y, by_x, cross_first, cross_second])
        return found

    def planes_of(found):
        planes = []
        for group in found:
            own, send = plane_lines(group)
            planes += [own, swap(send, "gx", 1)]
        return planes

    first = scaled(spectrum_of(*analyze(initial)))
    first_found = gather(first)
    second = scaled(again * first + spectrum_of(*analyze_product(initial)))
    second_found = gather(second)
    rate, *waves = next_rate(planes_of(first_found), initial)
    third = scaled(again * second + spectrum_of(*waves))
    third_found = gather(third)
    rate_again, *waves = next_rate(planes_of(second_found), rate)
    fourth = scaled(again * third + spectrum_of(*waves))
    fourth_found = gather(fourth)
    total = total_before(planes_of(third_found), rate, rate_again)
    total = total_last(planes_of(fourth_found), total)
    return total[None]


def solution(mesh):
    in_specs = (P("gx", "gy", None), P("gx", "gy", None))
    out_specs = P("lvl", "gx", "gy", None)
    return jax.shard_map(shards, mesh=mesh, in_specs=in_specs, out_specs=out_specs, check_vma=False)
```
